32 devices in a mesh: req: 16 (over z, y, x), tp: 2 (over core).
Axes of the slice: x: 2, y: 2, z: 4, core: 2. Of those that a mesh axis runs over, the one named last changes fastest.
Arguments:
- tokens: bfloat16 [2048, 2560], P('req'), may hold values from -6 to 6
- input_norm_gain: bfloat16 [2560], replicated, may hold values from 0.5 to 1.5
- query_weight: bfloat16 [2560, 4096], P(None, 'tp'), may hold values from -0.125 to 0.125
- key_value_weight: bfloat16 [2, 2560, 1024], P(None, None, 'tp'), may hold values from -0.125 to 0.125
- query_head_gain: bfloat16 [128], replicated, may hold values from 0.25 to 1.75
- key_head_gain: bfloat16 [128], replicated, may hold values from 0.25 to 1.75
- adapter_down_maps: bfloat16 [16, 48, 2560], P('req', None, 'tp'), may hold values from -0.125 to 0.125
- query_up_maps: bfloat16 [16, 16, 4096], P('req', None, 'tp'), may hold values from -0.75 to 0.75
- key_value_up_maps: bfloat16 [16, 2, 16, 1024], P('req', None, None, 'tp'), may hold values from -0.75 to 0.75
- packed_lengths: int32 [4], replicated, may hold values from 64 to 1024, as said below
- adapter_per_prompt: int32 [4], replicated, may hold values from 0 to 15, as said below
- adapter_place: int32 [16], replicated, may hold values from 0 to 15, each once
Outputs:
- attended: bfloat16 [2048, 4096], P('req', 'tp')
The draws below stay inside these ranges and needn't reach their ends.
Inputs may be any that keep to these rules, and one draw needn't show every extreme that they name: `packed_lengths`: every entry is a multiple of 64; exactly one is 1024, at least one is 64, and they sum to 2048. `adapter_per_prompt`: the prompts use distinct adapters.
All inputs are finite; a program needn't handle non-finite values.
Results may differ from the reference program's by a relative error of at most 0.0086.
Values may be sent and summed in bfloat16 or wider, within the bound.
A program may use at most 128 MiB of HBM per device.

```python
import math
import jax
import jax.numpy as jnp
from jax import lax

MODEL_WIDTH = 2560
QUERY_HEADS = 32
KEY_VALUE_HEADS = 8
HEAD_SIZE = 128
ADAPTER_RANK = 16
TOK_DEV = 128
SHORT_LEN = 64
ADAPTER_TOTAL = 16
PROMPTS = 4
TOKENS = 2048
LONG_LEN = 1024


def draw_packed_lengths(key, part):
    split_key = jax.random.fold_in(key, 21)
    order_key = jax.random.fold_in(key, 22)
    rest_units = (TOKENS - LONG_LEN) // SHORT_LEN
    unit_dev = TOK_DEV // SHORT_LEN
    top_pick = (rest_units - 3) // unit_dev + 1
    picked = jax.random.randint(split_key, (), 0, top_pick)
    first_units = 1 + unit_dev * picked
    last_units = rest_units - 1 - first_units
    swap_flag = jax.random.randint(order_key, (), 0, 2)
    third = jnp.where(swap_flag == 1, last_units, 1)
    fourth = jnp.where(swap_flag == 1, 1, last_units)
    lengths = jnp.stack([(first_units * SHORT_LEN).astype(jnp.int32), jnp.int32(LONG_LEN), (third * SHORT_LEN).astype(jnp.int32), (fourth * SHORT_LEN).astype(jnp.int32)])
    return lengths.astype(jnp.int32)


def draw_adapter_per_prompt(key, part):
    first_key = jax.random.fold_in(key, 11)
    return jax.random.permutation(first_key, ADAPTER_TOTAL)[:PROMPTS].astype(jnp.int32)


def block_levels(key, shape, split, low, largest):
    gain = 1.0
    for position, parts in split:
        steps = jax.random.uniform(jax.random.fold_in(jax.random.fold_in(key, 6), position), (parts,), jnp.float32, low / len(split), largest / len(split))
        gain = gain * jnp.repeat(jnp.exp(steps), shape[position] // parts).reshape((-1,) + (1,) * (len(shape) - 1 - position))
    return gain


def scatter_about(rng, shape, width, limit, cuts=(), kind=jnp.bfloat16):
    level = block_levels(rng, shape, cuts, -0.22, 0.18) if cuts else 1.0
    drawn = jax.random.normal(rng, shape, jnp.float32) * width * level
    return jnp.minimum(jnp.maximum(drawn, -limit), limit).astype(kind)


def setup_inputs(seed: int = 0) -> dict:
    key_list = jax.random.split(jax.random.key(seed), 13)
    return {
        "tokens": scatter_about(key_list[0], (TOKENS, MODEL_WIDTH), 1.0, 6.0, ((0, 16),)),
        "input_norm_gain": jnp.clip(1.0 + 0.1 * jax.random.normal(key_list[1], (MODEL_WIDTH,), jnp.float32), 0.5, 1.5).astype(jnp.bfloat16),
        "query_weight": scatter_about(key_list[2], (MODEL_WIDTH, QUERY_HEADS * HEAD_SIZE), MODEL_WIDTH ** -0.5, 0.125, ((1, 2),)),
        "key_value_weight": scatter_about(key_list[3], (2, MODEL_WIDTH, KEY_VALUE_HEADS * HEAD_SIZE), MODEL_WIDTH ** -0.5, 0.125, ((2, 2),)),
        "query_head_gain": jnp.clip(1.0 + 0.15 * jax.random.normal(key_list[4], (HEAD_SIZE,), jnp.float32), 0.25, 1.75).astype(jnp.bfloat16),
        "key_head_gain": jnp.clip(1.0 + 0.15 * jax.random.normal(key_list[5], (HEAD_SIZE,), jnp.float32), 0.25, 1.75).astype(jnp.bfloat16),
        "adapter_down_maps": scatter_about(key_list[6], (ADAPTER_TOTAL, 3 * ADAPTER_RANK, MODEL_WIDTH), MODEL_WIDTH ** -0.5, 0.125, ((0, 16), (2, 2))),
        "query_up_maps": scatter_about(key_list[7], (ADAPTER_TOTAL, ADAPTER_RANK, QUERY_HEADS * HEAD_SIZE), (4 * ADAPTER_RANK) ** -0.5, 0.75, ((0, 16), (2, 2))),
        "key_value_up_maps": scatter_about(key_list[8], (ADAPTER_TOTAL, 2, ADAPTER_RANK, KEY_VALUE_HEADS * HEAD_SIZE), (4 * ADAPTER_RANK) ** -0.5, 0.75, ((0, 16), (3, 2))),
        "packed_lengths": draw_packed_lengths(jax.random.fold_in(key_list[12], 71), 0),
        "adapter_per_prompt": draw_adapter_per_prompt(jax.random.fold_in(key_list[12], 71), 0),
        "adapter_place": jax.random.permutation(key_list[11], ADAPTER_TOTAL).astype(jnp.int32),
    }


epsilon = 1e-06
theta = 1000000.0
adapter_scale = 2.0

def normalize(values, gain_vec):
    values = values.astype(jnp.float32)
    inverse = lax.rsqrt(lax.optimization_barrier(jnp.mean(values * values, axis=-1, keepdims=True)) + epsilon)
    return values * inverse * gain_vec.astype(jnp.float32)

def rotate(values, offsets):
    half_dim = values.shape[-1] // 2
    powers = jnp.arange(half_dim, dtype=jnp.float32) * (2.0 / values.shape[-1])
    frequency = theta ** (-powers)
    angles = offsets.astype(jnp.float32)[:, None] * frequency[None, :]
    cosine = jnp.cos(angles)[:, None, :]
    sine_part = jnp.sin(angles)[:, None, :]
    former = values[..., :half_dim]
    latter = values[..., half_dim:]
    return jnp.concatenate([former * cosine - latter * sine_part, latter * cosine + former * sine_part], axis=-1)

def doc_start(positions, packed_lengths):
    doc_end = jnp.cumsum(packed_lengths).astype(jnp.int32)
    return lax.optimization_barrier(jnp.sum(jnp.where(doc_end[None, :] <= positions[:, None], packed_lengths[None, :], 0), axis=1)).astype(jnp.int32)

def holders(positions, packed_lengths, adapter_per_prompt, adapter_place):
    doc_end = jnp.cumsum(packed_lengths).astype(jnp.int32)
    inside = (doc_end[None, :] > positions[:, None]) & (doc_end[None, :] - packed_lengths[None, :] <= positions[:, None])
    adapter = lax.optimization_barrier(jnp.sum(jnp.where(inside, adapter_per_prompt[None, :], 0), axis=1)).astype(jnp.int32)
    catalog = jnp.arange(adapter_place.shape[0], dtype=jnp.int32)
    return lax.optimization_barrier(jnp.sum(jnp.where(adapter[:, None] == catalog[None, :], adapter_place[None, :], 0), axis=1)).astype(jnp.int32)

def reference(tokens, input_norm_gain, query_weight, key_value_weight, query_head_gain, key_head_gain, adapter_down_maps, query_up_maps, key_value_up_maps, packed_lengths, adapter_per_prompt, adapter_place):
    token_total = tokens.shape[0]
    positions = jnp.arange(token_total, dtype=jnp.int32)
    starts = doc_start(positions, packed_lengths)
    owners = holders(positions, packed_lengths, adapter_per_prompt, adapter_place)
    normed = normalize(tokens, input_norm_gain).astype(jnp.bfloat16)
    plain_query = jnp.dot(normed, query_weight, preferred_element_type=jnp.float32)
    plain_key = jnp.dot(normed, key_value_weight[0], preferred_element_type=jnp.float32)
    plain_value = jnp.dot(normed, key_value_weight[1], preferred_element_type=jnp.float32)
    unit_count = token_total // SHORT_LEN

    def adapt_unit(unit_entry):
        piece_rows, keeper = unit_entry
        reduced_rank = jnp.dot(piece_rows, adapter_down_maps[keeper].T, preferred_element_type=jnp.float32).astype(jnp.bfloat16)
        query_increment = jnp.dot(reduced_rank[:, :ADAPTER_RANK], query_up_maps[keeper], preferred_element_type=jnp.float32)
        key_increment = jnp.dot(reduced_rank[:, ADAPTER_RANK:2 * ADAPTER_RANK], key_value_up_maps[keeper, 0], preferred_element_type=jnp.float32)
        value_increment = jnp.dot(reduced_rank[:, 2 * ADAPTER_RANK:], key_value_up_maps[keeper, 1], preferred_element_type=jnp.float32)
        return (query_increment, key_increment, value_increment)
    query_increment, key_increment, value_increment = lax.map(adapt_unit, (normed.reshape(unit_count, SHORT_LEN, MODEL_WIDTH), owners[::SHORT_LEN]))
    offsets = positions - starts
    query_every_token = (plain_query + adapter_scale * query_increment.reshape(token_total, -1)).reshape(token_total, QUERY_HEADS, HEAD_SIZE)
    query_every_token = rotate(normalize(query_every_token, query_head_gain), offsets).astype(jnp.bfloat16)
    key_every_token = (plain_key + adapter_scale * key_increment.reshape(token_total, -1)).reshape(token_total, KEY_VALUE_HEADS, HEAD_SIZE)
    key_every_token = rotate(normalize(key_every_token, key_head_gain), offsets).astype(jnp.bfloat16)
    value_every_token = (plain_value + adapter_scale * value_increment.reshape(token_total, -1)).reshape(token_total, KEY_VALUE_HEADS, HEAD_SIZE).astype(jnp.bfloat16)
    group_width = QUERY_HEADS // KEY_VALUE_HEADS
    query_rows = math.gcd(token_total, 512)
    key_span = min(token_total, LONG_LEN + query_rows)

    def attend_block(block_index):
        block_first = (block_index * query_rows).astype(jnp.int32)
        queries = lax.dynamic_slice_in_dim(query_every_token, block_first, query_rows, 0)
        query_pos = block_first + jnp.arange(query_rows, dtype=jnp.int32)
        query_start = lax.dynamic_slice_in_dim(starts, block_first, query_rows, 0)
        key_first = jnp.clip(block_first + query_rows - key_span, 0, token_total - key_span).astype(jnp.int32)
        key_block = lax.dynamic_slice_in_dim(key_every_token, key_first, key_span, 0)
        value_block = lax.dynamic_slice_in_dim(value_every_token, key_first, key_span, 0)
        key_pos = key_first + jnp.arange(key_span, dtype=jnp.int32)
        key_start = lax.dynamic_slice_in_dim(starts, key_first, key_span, 0)
        visible = (key_start[None, :] == query_start[:, None]) & (key_pos[None, :] <= query_pos[:, None])

        def head_attention(kv_index):
            head_queries = lax.dynamic_slice_in_dim(queries, kv_index * group_width, group_width, 1).astype(jnp.float32)
            head_keys = lax.dynamic_index_in_dim(key_block, kv_index, 1, keepdims=False).astype(jnp.float32)
            head_values = lax.dynamic_index_in_dim(value_block, kv_index, 1, keepdims=False).astype(jnp.float32)
            scores = jnp.einsum('tgd,sd->gts', head_queries, head_keys) / math.sqrt(HEAD_SIZE)
            weights = jnp.where(visible[None], jnp.exp(scores), 0.0)
            totals = lax.optimization_barrier(jnp.sum(weights, axis=-1))
            rounded = lax.optimization_barrier(weights.astype(jnp.bfloat16)).astype(jnp.float32)
            numerator = jnp.einsum('gts,sd->gtd', rounded, head_values)
            return numerator / totals[..., None]
        output_rows = lax.map(head_attention, jnp.arange(KEY_VALUE_HEADS, dtype=jnp.int32))
        return output_rows.transpose(2, 0, 1, 3).reshape(query_rows, QUERY_HEADS * HEAD_SIZE)
    attended = lax.map(attend_block, jnp.arange(token_total // query_rows, dtype=jnp.int32))
    return attended.reshape(token_total, QUERY_HEADS * HEAD_SIZE).astype(jnp.bfloat16)
```

```python
import functools
import math

import jax
import jax.numpy as jnp
import numpy as np
from jax import lax
from jax.experimental import pallas as pl
from jax.experimental.pallas import tpu as pltpu
from jax.sharding import PartitionSpec as P

SHORT_LEN = 64
PLANE = 4
EPSILON = 1e-06
THETA = 1000000.0
ADAPTER_SCALE = 2.0
MASKED = -1e30
MESH = pl.DeviceIdType.MESH


def nt_dot(left, right):
    return lax.dot_general(
        left, right, (((1,), (1,)), ((), ())), preferred_element_type=jnp.float32
    )


def fused_kernel(
    cfg,
    lengths_ref,
    prompt_adapter_ref,
    place_ref,
    tokens_ref,
    gain_ref,
    qgain_ref,
    kgain_ref,
    freq_ref,
    down_ref,
    upq_ref,
    upkv_ref,
    wq_hbm,
    wkv_hbm,
    out_ref,
    wq,
    wkv,
    xn,
    xown,
    slab,
    part1,
    stage2,
    maps,
    dmaps,
    lowp,
    lowr,
    plain_q,
    plain_kv,
    qbuf,
    kvb,
    acc,
    accl,
    cos_t,
    sin_t,
    wq_sem,
    wkv_sem,
    s1_sem,
    r1_sem,
    s2_sem,
    r2_sem,
    sl_sem,
    rl_sem,
    zs_sem,
    zr_sem,
    ps_sem,
    pr_sem,
):
    n, tpn, rows, units = cfg["n"], cfg["tpn"], cfg["rows"], cfg["units"]
    rank, lw, dseg, piece, pieces = (
        cfg["rank"],
        cfg["lw"],
        cfg["dseg"],
        cfg["piece"],
        cfg["pieces"],
    )
    nkv, group, hw = cfg["nkv"], cfg["group"], cfg["hw"]
    kvw, gw = nkv * hw, group * hw
    planes, back = n // PLANE, n // 2 // PLANE
    me = lax.axis_index("req")
    tp = lax.axis_index("tp")
    hi = lax.div(me, PLANE)
    lo = lax.rem(me, PLANE)

    def q_copy(c):
        return pltpu.make_async_copy(
            wq_hbm.at[:, pl.ds(pl.multiple_of(c * gw, 128), gw)], wq.at[c], wq_sem.at[c]
        )

    def kv_copy(c):
        return pltpu.make_async_copy(wkv_hbm.at[c], wkv.at[c], wkv_sem.at[c])

    for c in range(2):
        kv_copy(c).start()
    for c in range(nkv):
        q_copy(c).start()

    barrier = pltpu.get_barrier_semaphore()

    def greet(k, carry):
        pl.semaphore_signal(
            barrier, inc=1, device_id=(lax.rem(me + k, n), tp), device_id_type=MESH
        )
        return carry

    lax.fori_loop(1, n, greet, 0)
    for k in range(1, tpn):
        pl.semaphore_signal(
            barrier, inc=1, device_id=(me, lax.rem(tp + k, tpn)), device_id_type=MESH
        )

    if dseg > lw:
        slab[...] = jnp.zeros_like(slab)
    for r in range(3):
        slab[:, r * dseg : r * dseg + lw] = down_ref[0, r * rank : (r + 1) * rank, :]
    base = 3 * dseg
    slab[:, base : base + nkv * gw] = upq_ref[0]
    for c in range(2):
        at = base + nkv * gw + c * kvw
        slab[:, at : at + kvw] = upkv_ref[0, c]
    used = base + nkv * gw + 2 * kvw
    if pieces * piece > used:
        slab[:, used:] = jnp.zeros((rank, pieces * piece - used), slab.dtype)

    pl.semaphore_wait(barrier, n - 1 + tpn - 1)

    def lanes(index):
        return pl.ds(pl.multiple_of(index * piece, 128), piece)

    def first_copy(dest, source):
        return pltpu.make_async_remote_copy(
            src_ref=slab.at[:, lanes(dest)],
            dst_ref=part1.at[source],
            send_sem=s1_sem.at[dest],
            recv_sem=r1_sem.at[source],
            device_id=(dest, tp),
            device_id_type=MESH,
        )

    def first_send(k, carry):
        dest = lax.rem(me + k, n)

        @pl.when(dest < pieces)
        def _():
            first_copy(dest, me).start()

        return carry

    lax.fori_loop(1, n, first_send, 0)

    values = tokens_ref[...].astype(jnp.float32)
    inverse = lax.rsqrt(jnp.mean(values * values, axis=-1, keepdims=True) + EPSILON)
    xn[...] = (values * inverse * gain_ref[...].astype(jnp.float32)).astype(jnp.bfloat16)
    if dseg > lw:
        xown[...] = jnp.zeros_like(xown)
    for k in range(tpn):

        @pl.when(tp == k)
        def _():
            xown[:, :lw] = xn[:, k * lw : (k + 1) * lw]

    def kv_product(c, carry):
        kv_copy(c).wait()
        plain_kv[c] = jnp.dot(xn[...], wkv[c], preferred_element_type=jnp.float32)
        return carry

    lax.fori_loop(0, 2, kv_product, 0)

    count = lengths_ref.shape[0]
    ends = []
    running = jnp.int32(0)
    for j in range(count):
        running = running + lengths_ref[j]
        ends.append(running)

    def slot_of(position):
        prompt = jnp.int32(0)
        for j in range(count - 1):
            prompt = prompt + (ends[j] <= position).astype(jnp.int32)
        return place_ref[prompt_adapter_ref[prompt]]

    def second_copy(dest, source):
        return pltpu.make_async_remote_copy(
            src_ref=stage2.at[dest],
            dst_ref=maps.at[:, :, lanes(source)],
            send_sem=s2_sem.at[dest],
            recv_sem=r2_sem.at[source],
            device_id=(dest, tp),
            device_id_type=MESH,
        )

    @pl.when(me < pieces)
    def _():
        part1[me] = slab[:, lanes(me)]

        def first_wait(k, carry):
            source = lax.rem(me + k, n)
            first_copy(me, source).wait_recv()
            return carry

        lax.fori_loop(1, n, first_wait, 0)

        def second_send(k, carry):
            dest = lax.rem(me + k, n)
            for u in range(units):
                stage2[dest, u] = part1[slot_of((dest * units + u) * SHORT_LEN)]
            second_copy(dest, me).start()
            return carry

        lax.fori_loop(1, n, second_send, 0)
        for u in range(units):
            maps[u, :, lanes(me)] = part1[slot_of((me * units + u) * SHORT_LEN)]

    def q_product(c, carry):
        q_copy(c).wait()
        plain_q[c] = jnp.dot(xn[...], wq[c], preferred_element_type=jnp.float32)
        return carry

    lax.fori_loop(0, nkv, q_product, 0)

    row_pos = me * rows + lax.broadcasted_iota(jnp.int32, (rows, hw), 0)
    row_start = jnp.zeros((rows, hw), jnp.int32)
    for j in range(count):
        row_start = row_start + jnp.where(ends[j] <= row_pos, lengths_ref[j], 0)
    angles = (row_pos - row_start).astype(jnp.float32) * freq_ref[...]
    sine = jnp.sin(angles)
    cos_t[...] = jnp.cos(angles)
    lane = lax.broadcasted_iota(jnp.int32, (rows, hw), 1)
    sin_t[...] = jnp.where(lane < hw // 2, -sine, sine)
    dmaps[...] = jnp.zeros_like(dmaps)
    acc[...] = jnp.zeros_like(acc)
    accl[...] = jnp.zeros_like(accl)

    def second_wait(k, carry):
        source = lax.rem(me + k, n)

        @pl.when(source < pieces)
        def _():
            second_copy(me, source).wait_recv()

        return carry

    lax.fori_loop(1, n, second_wait, 0)

    for u in range(units):
        for r in range(3):
            dmaps[u, r * rank : (r + 1) * rank, :] = maps[u, :, r * dseg : (r + 1) * dseg]
        rows_u = slice(u * SHORT_LEN, (u + 1) * SHORT_LEN)
        lowp[rows_u, :] = nt_dot(xown[rows_u, :], dmaps[u])

    def low_copy(k, source):
        return pltpu.make_async_remote_copy(
            src_ref=lowp,
            dst_ref=lowr.at[source],
            send_sem=sl_sem.at[k],
            recv_sem=rl_sem.at[source],
            device_id=(me, lax.rem(tp + k, tpn)),
            device_id_type=MESH,
        )

    for k in range(1, tpn):
        low_copy(k, tp).start()
    low = lowp[...]
    for k in range(1, tpn):
        source = lax.rem(tp + k, tpn)
        low_copy(tpn - k, source).wait_recv()
        low = low + lowr[source]
    low = low.astype(jnp.bfloat16)

    def increment(part, start, width):
        return [
            jnp.dot(
                low[u * SHORT_LEN : (u + 1) * SHORT_LEN, part * rank : (part + 1) * rank],
                maps[u, :, pl.ds(start, width)],
                preferred_element_type=jnp.float32,
            )
            for u in range(units)
        ]

    def head(values, gain):
        inverse = lax.rsqrt(jnp.mean(values * values, axis=-1, keepdims=True) + EPSILON)
        values = values * inverse * gain
        return (values * cos_t[...] + pltpu.roll(values, hw // 2, 1) * sin_t[...]).astype(
            jnp.bfloat16
        )

    kgain = kgain_ref[...].astype(jnp.float32)
    qgain = qgain_ref[...].astype(jnp.float32)
    k_at = base + nkv * gw
    k_raw = plain_kv[0] + ADAPTER_SCALE * jnp.concatenate(increment(1, k_at, kvw), 0)
    v_raw = plain_kv[1] + ADAPTER_SCALE * jnp.concatenate(increment(2, k_at + kvw, kvw), 0)
    for k in range(nkv):
        kvb[0, lo, 0, :, k * hw : (k + 1) * hw] = head(k_raw[:, k * hw : (k + 1) * hw], kgain)
    kvb[0, lo, 1] = v_raw.astype(jnp.bfloat16)

    xn_lo = lo + 1 - 2 * lax.rem(lo, 2)
    yn_lo = lax.rem(lo + 2, PLANE)
    dn_lo = PLANE - 1 - lo

    def need(s, source, dest):
        if s == 0:
            return source < dest
        if s == back:
            return source > dest
        return source >= 0

    def z_copy(s):
        return pltpu.make_async_remote_copy(
            src_ref=kvb.at[s, lo],
            dst_ref=kvb.at[s + 1, lo],
            send_sem=zs_sem.at[s],
            recv_sem=zr_sem.at[s + 1],
            device_id=(lax.rem(me + PLANE, n), tp),
            device_id_type=MESH,
        )

    def p_copy(kind, s, block, half, dest):
        return pltpu.make_async_remote_copy(
            src_ref=kvb.at[s, block, half],
            dst_ref=kvb.at[s, block, half],
            send_sem=ps_sem.at[kind, s],
            recv_sem=pr_sem.at[kind, s],
            device_id=(hi * PLANE + dest, tp),
            device_id_type=MESH,
        )

    def plan(s, sender, x_of, y_of, d_of):
        return (
            (0, sender, 0, x_of, need(s, sender, x_of)),
            (1, sender, 1, x_of, need(s, sender, x_of) | need(s, sender, d_of)),
            (2, sender, 0, y_of, need(s, sender, y_of) | need(s, sender, d_of)),
            (3, sender, 1, y_of, need(s, sender, y_of)),
        )

    def relays(s):
        return (
            (4, yn_lo, 0, xn_lo, need(s, yn_lo, xn_lo)),
            (5, xn_lo, 1, yn_lo, need(s, xn_lo, yn_lo)),
        )

    def launch(s):
        if s < back:

            @pl.when((hi >= s) & (hi + 1 < planes))
            def _():
                z_copy(s).start()

        for kind, block, half, dest, wanted in plan(s, lo, xn_lo, yn_lo, dn_lo):

            @pl.when((hi >= s) & wanted)
            def _():
                p_copy(kind, s, block, half, dest).start()

    def arrive(s):
        from_x = plan(s, xn_lo, lo, dn_lo, yn_lo)[:2]
        from_y = plan(s, yn_lo, dn_lo, lo, xn_lo)[2:]
        for (kind, block, half, dest, wanted), relay in zip(
            (from_y[0], from_x[1], from_x[0], from_y[1]), relays(s) + (None, None)
        ):

            @pl.when((hi >= s) & wanted)
            def _():
                p_copy(kind, s, block, half, dest).wait_recv()

            if relay is not None:
                r_kind, r_block, r_half, r_dest, r_wanted = relay

                @pl.when((hi >= s) & r_wanted)
                def _():
                    p_copy(r_kind, s, r_block, r_half, r_dest).start()

    def diagonal(s):
        @pl.when((hi >= s) & need(s, dn_lo, lo))
        def _():
            p_copy(4, s, dn_lo, 0, lo).wait_recv()
            p_copy(5, s, dn_lo, 1, lo).wait_recv()

    factor = math.log2(math.e) / math.sqrt(hw)

    def attend(s, block, wanted):
        @pl.when((hi >= s) & wanted)
        def _():
            key_pos = ((hi - s) * PLANE + block) * rows + lax.broadcasted_iota(
                jnp.int32, (rows, rows), 1
            )
            query_pos = me * rows + lax.broadcasted_iota(jnp.int32, (rows, rows), 0)
            first = jnp.zeros((rows, rows), jnp.int32)
            for j in range(count):
                first = first + jnp.where(ends[j] <= query_pos, lengths_ref[j], 0)
            bias = jnp.where((key_pos >= first) & (key_pos <= query_pos), 0.0, MASKED)
            bias = jnp.concatenate([bias] * group, 0)
            for k in range(nkv):
                cols = slice(k * hw, (k + 1) * hw)
                weights = jnp.exp2(nt_dot(qbuf[k], kvb[s, block, 0, :, cols]) * factor + bias)
                accl[k] += weights
                acc[k] += jnp.dot(
                    weights.astype(jnp.bfloat16),
                    kvb[s, block, 1, :, cols],
                    preferred_element_type=jnp.float32,
                )

    launch(0)

    def q_final(c, carry):
        start = pl.multiple_of(base + c * gw, 128)
        raw = plain_q[c] + ADAPTER_SCALE * jnp.concatenate(increment(0, start, gw), 0)
        for g in range(group):
            qbuf[c, g * rows : (g + 1) * rows, :] = head(raw[:, g * hw : (g + 1) * hw], qgain)
        return carry

    lax.fori_loop(0, nkv, q_final, 0)

    for s in range(back + 1):
        if s < back:

            @pl.when(hi >= s + 1)
            def _():
                z_copy(s).wait_recv()

            launch(s + 1)
        arrive(s)
        attend(s, lo, lo >= 0)
        attend(s, xn_lo, need(s, xn_lo, lo))
        attend(s, yn_lo, need(s, yn_lo, lo))
        if s >= 1:
            diagonal(s - 1)
            attend(s - 1, dn_lo, need(s - 1, dn_lo, lo))
    diagonal(back)
    attend(back, dn_lo, need(back, dn_lo, lo))

    for k in range(nkv):
        total = jnp.sum(accl[k], axis=-1, keepdims=True)
        result = (acc[k] / total).astype(out_ref.dtype)
        for g in range(group):
            at = (k * group + g) * hw
            out_ref[:, at : at + hw] = result[g * rows : (g + 1) * rows, :]

    def drain(k, carry):
        dest = lax.rem(me + k, n)

        @pl.when(dest < pieces)
        def _():
            first_copy(dest, me).wait_send()

        @pl.when(me < pieces)
        def _():
            second_copy(dest, me).wait_send()

        return carry

    lax.fori_loop(1, n, drain, 0)
    for k in range(1, tpn):
        low_copy(k, tp).wait_send()
    for s in range(back + 1):
        if s < back:

            @pl.when((hi >= s) & (hi + 1 < planes))
            def _():
                z_copy(s).wait_send()

        for kind, block, half, dest, wanted in (
            plan(s, lo, xn_lo, yn_lo, dn_lo) + relays(s)
        ):

            @pl.when((hi >= s) & wanted)
            def _():
                p_copy(kind, s, block, half, dest).wait_send()


def on_device(
    n,
    tpn,
    tokens,
    input_norm_gain,
    query_weight,
    key_value_weight,
    query_head_gain,
    key_head_gain,
    adapter_down_maps,
    query_up_maps,
    key_value_up_maps,
    packed_lengths,
    adapter_per_prompt,
    adapter_place,
):
    rows, width = tokens.shape
    hw = query_head_gain.shape[0]
    nkv = key_value_weight.shape[2] // hw
    group = query_weight.shape[1] // hw // nkv
    rank, lw = query_up_maps.shape[1], adapter_down_maps.shape[2]
    units = rows // SHORT_LEN
    dseg = -(-lw // 128) * 128
    kvw, gw = nkv * hw, group * hw
    used = 3 * dseg + nkv * gw + 2 * kvw
    tiles = used // 128
    piece = -(-tiles // n) * 128
    pieces = -(-used // piece)
    back = n // 2 // PLANE
    cfg = dict(
        n=n,
        tpn=tpn,
        rows=rows,
        units=units,
        rank=rank,
        lw=lw,
        dseg=dseg,
        piece=piece,
        pieces=pieces,
        nkv=nkv,
        group=group,
        hw=hw,
    )
    powers = np.arange(hw // 2, dtype=np.float64) * (2.0 / hw)
    frequency = (THETA ** (-powers)).astype(np.float32)
    frequency = jnp.asarray(np.concatenate([frequency, frequency])[None, :])
    smem = pl.BlockSpec(memory_space=pltpu.SMEM)
    vmem = pl.BlockSpec(memory_space=pltpu.VMEM)
    hbm = pl.BlockSpec(memory_space=pl.ANY)
    bf, f32 = jnp.bfloat16, jnp.float32
    dma = pltpu.SemaphoreType.DMA
    call = pl.pallas_call(
        functools.partial(fused_kernel, cfg),
        out_shape=jax.ShapeDtypeStruct((rows, nkv * gw), bf),
        in_specs=[smem] * 3 + [vmem] * 8 + [hbm] * 2,
        out_specs=vmem,
        scratch_shapes=[
            pltpu.VMEM((nkv, width, gw), bf),
            pltpu.VMEM((2, width, kvw), bf),
            pltpu.VMEM((rows, width), bf),
            pltpu.VMEM((rows, dseg), bf),
            pltpu.VMEM((rank, pieces * piece), bf),
            pltpu.VMEM((n, rank, piece), bf),
            pltpu.VMEM((n, units, rank, piece), bf),
            pltpu.VMEM((units, rank, pieces * piece), bf),
            pltpu.VMEM((units, 128, dseg), bf),
            pltpu.VMEM((rows, 128), f32),
            pltpu.VMEM((tpn, rows, 128), f32),
            pltpu.VMEM((nkv, rows, gw), f32),
            pltpu.VMEM((2, rows, kvw), f32),
            pltpu.VMEM((nkv, group * rows, hw), bf),
            pltpu.VMEM((back + 1, PLANE, 2, rows, kvw), bf),
            pltpu.VMEM((nkv, group * rows, hw), f32),
            pltpu.VMEM((nkv, group * rows, rows), f32),
            pltpu.VMEM((rows, hw), f32),
            pltpu.VMEM((rows, hw), f32),
            dma((nkv,)),
            dma((2,)),
            dma((n,)),
            dma((n,)),
            dma((n,)),
            dma((n,)),
            dma((tpn,)),
            dma((tpn,)),
            dma((back + 1,)),
            dma((back + 1,)),
            dma((6, back + 1)),
            dma((6, back + 1)),
        ],
        compiler_params=pltpu.CompilerParams(
            collective_id=0, has_side_effects=True, vmem_limit_bytes=50 << 20
        ),
    )
    return call(
        packed_lengths,
        adapter_per_prompt,
        adapter_place,
        tokens,
        input_norm_gain.reshape(1, -1),
        query_head_gain.reshape(1, -1),
        key_head_gain.reshape(1, -1),
        frequency,
        adapter_down_maps,
        query_up_maps,
        key_value_up_maps,
        query_weight,
        key_value_weight,
    )


def solution(mesh):
    in_specs = (
        P("req", None),
        P(),
        P(None, "tp"),
        P(None, None, "tp"),
        P(),
        P(),
        P("req", None, "tp"),
        P("req", None, "tp"),
        P("req", None, None, "tp"),
        P(),
        P(),
        P(),
    )
    body = functools.partial(on_device, mesh.shape["req"], mesh.shape["tp"])
    return jax.shard_map(
        body, mesh=mesh, in_specs=in_specs, out_specs=P("req", "tp"), check_vma=False
    )
```

```python
import functools
import math

import jax
import jax.numpy as jnp
import numpy as np
from jax import lax
from jax.experimental import pallas as pl
from jax.experimental.pallas import tpu as pltpu
from jax.sharding import PartitionSpec as P

SHORT_LEN = 64
PLANE = 4
EPSILON = 1e-06
THETA = 1000000.0
ADAPTER_SCALE = 2.0
MASKED = -1e30
MESH = pl.DeviceIdType.MESH


def nt_dot(left, right):
    return lax.dot_general(
        left, right, (((1,), (1,)), ((), ())), preferred_element_type=jnp.float32
    )


def fused_kernel(
    cfg,
    lengths_hbm,
    prompt_adapter_hbm,
    place_hbm,
    tokens_hbm,
    gain_hbm,
    qgain_hbm,
    kgain_hbm,
    freq_hbm,
    down_hbm,
    upq_hbm,
    upkv_hbm,
    wq_hbm,
    wkv_hbm,
    out_ref,
    lengths_ref,
    prompt_adapter_ref,
    place_ref,
    tokens_ref,
    gain_ref,
    qgain_ref,
    kgain_ref,
    freq_ref,
    down_ref,
    upq_ref,
    upkv_ref,
    wq,
    wkv,
    xn,
    xown,
    slab_a,
    slab_b,
    part_a,
    part_b,
    stage_a,
    stage_b,
    maps_a,
    maps_b,
    dmaps,
    lowp,
    lowr,
    plain_q,
    plain_k,
    qbuf,
    kb0,
    kb1,
    vb0,
    vb1,
    acc,
    accl,
    accd,
    cos_t,
    sin_t,
    in_sem,
    wq_sem,
    wkv_sem,
    s1_sem,
    r1_sem,
    s2_sem,
    r2_sem,
    sl_sem,
    rl_sem,
    zs_sem,
    zr_sem,
    ps_sem,
    pr_sem,
):
    n, tpn, rows, units = cfg["n"], cfg["tpn"], cfg["rows"], cfg["units"]
    rank, lw, dseg = cfg["rank"], cfg["lw"], cfg["dseg"]
    nkv, group, hw = cfg["nkv"], cfg["group"], cfg["hw"]
    kvw, gw, half_rows = nkv * hw, group * hw, rows // 2
    planes, back = n // PLANE, n // 2 // PLANE
    me = lax.axis_index("req")
    tp = lax.axis_index("tp")
    hi = lax.div(me, PLANE)
    lo = lax.rem(me, PLANE)

    def q_copy(c):
        return pltpu.make_async_copy(
            wq_hbm.at[:, pl.ds(pl.multiple_of(c * gw, 128), gw)], wq.at[c], wq_sem.at[c]
        )

    def kv_copy(c):
        return pltpu.make_async_copy(wkv_hbm.at[c], wkv.at[c], wkv_sem.at[c])

    loads = [
        pltpu.make_async_copy(source, dest, in_sem.at[i])
        for i, (source, dest) in enumerate(
            (
                (down_hbm, down_ref),
                (upkv_hbm, upkv_ref),
                (upq_hbm, upq_ref),
                (tokens_hbm, tokens_ref),
                (gain_hbm, gain_ref),
                (lengths_hbm, lengths_ref),
                (prompt_adapter_hbm, prompt_adapter_ref),
                (place_hbm, place_ref),
                (freq_hbm, freq_ref),
                (qgain_hbm, qgain_ref),
                (kgain_hbm, kgain_ref),
            )
        )
    ]
    for load in loads:
        load.start()
    kv_copy(1).start()
    kv_copy(0).start()
    for c in range(nkv):
        q_copy(c).start()

    barrier = pltpu.get_barrier_semaphore()

    def greet(k, carry):
        pl.semaphore_signal(
            barrier, inc=1, device_id=(lax.rem(me + k, n), tp), device_id_type=MESH
        )
        return carry

    lax.fori_loop(1, n, greet, 0)
    for k in range(1, tpn):
        pl.semaphore_signal(
            barrier, inc=1, device_id=(me, lax.rem(tp + k, tpn)), device_id_type=MESH
        )
    for load in loads[:3]:
        load.wait()

    slab_a[...] = jnp.zeros_like(slab_a)
    slab_b[...] = jnp.zeros_like(slab_b)
    slab_b[:, :lw] = down_ref[0, :rank, :]
    slab_a[:, :lw] = down_ref[0, rank : 2 * rank, :]
    slab_a[:, dseg : dseg + lw] = down_ref[0, 2 * rank : 3 * rank, :]
    k_at, q_at = 2 * dseg, dseg
    v_at = q_at + nkv * gw
    slab_a[:, k_at : k_at + kvw] = upkv_ref[0, 0]
    slab_b[:, q_at : q_at + nkv * gw] = upq_ref[0]
    slab_b[:, v_at : v_at + kvw] = upkv_ref[0, 1]

    pl.semaphore_wait(barrier, n - 1 + tpn - 1)

    groups = (
        (slab_a, part_a, stage_a, maps_a, cfg["piece_a"], cfg["pieces_a"]),
        (slab_b, part_b, stage_b, maps_b, cfg["piece_b"], cfg["pieces_b"]),
    )

    def lanes(index, piece):
        return pl.ds(pl.multiple_of(index * piece, 128), piece)

    def first_copy(x, dest, source):
        slab, part, _, _, piece, _ = groups[x]
        return pltpu.make_async_remote_copy(
            src_ref=slab.at[:, lanes(dest, piece)],
            dst_ref=part.at[source],
            send_sem=s1_sem.at[x, dest],
            recv_sem=r1_sem.at[x, source],
            device_id=(dest, tp),
            device_id_type=MESH,
        )

    def first_phase(x):
        def first_send(k, carry):
            dest = lax.rem(me + k, n)

            @pl.when(dest < groups[x][5])
            def _():
                first_copy(x, dest, me).start()

            return carry

        lax.fori_loop(1, n, first_send, 0)

    first_phase(0)
    first_phase(1)

    for load in loads[3:]:
        load.wait()
    count = cfg["count"]
    lengths = [lengths_ref[j] for j in range(count)]
    ends = []
    running = jnp.int32(0)
    for j in range(count):
        running = running + lengths[j]
        ends.append(running)

    values = tokens_ref[...].astype(jnp.float32)
    inverse = lax.rsqrt(jnp.mean(values * values, axis=-1, keepdims=True) + EPSILON)
    xn[...] = (values * inverse * gain_ref[...].astype(jnp.float32)).astype(jnp.bfloat16)
    kv_copy(1).wait()
    plain_v = jnp.dot(xn[...], wkv[1], preferred_element_type=jnp.float32).astype(jnp.bfloat16)
    vb0[0, lo] = plain_v[:half_rows]
    vb1[0, lo] = plain_v[half_rows:]

    def slot_of(position):
        prompt = jnp.int32(0)
        for j in range(count - 1):
            prompt = prompt + (ends[j] <= position).astype(jnp.int32)
        return place_ref[prompt_adapter_ref[prompt]]

    def second_copy(x, dest, source):
        _, _, stage, maps, piece, _ = groups[x]
        return pltpu.make_async_remote_copy(
            src_ref=stage.at[dest],
            dst_ref=maps.at[:, :, lanes(source, piece)],
            send_sem=s2_sem.at[x, dest],
            recv_sem=r2_sem.at[x, source],
            device_id=(dest, tp),
            device_id_type=MESH,
        )

    def second_phase(x):
        slab, part, stage, maps, piece, pieces = groups[x]

        @pl.when(me < pieces)
        def _():
            part[me] = slab[:, lanes(me, piece)]

            def first_wait(k, carry):
                first_copy(x, me, lax.rem(me + k, n)).wait_recv()
                return carry

            lax.fori_loop(1, n, first_wait, 0)

            def second_send(k, carry):
                dest = lax.rem(me + k, n)
                for u in range(units):
                    stage[dest, u] = part[slot_of((dest * units + u) * SHORT_LEN)]
                second_copy(x, dest, me).start()
                return carry

            lax.fori_loop(1, n, second_send, 0)
            for u in range(units):
                maps[u, :, lanes(me, piece)] = part[slot_of((me * units + u) * SHORT_LEN)]

    def second_arrival(x):
        def second_wait(k, carry):
            source = lax.rem(me + k, n)

            @pl.when(source < groups[x][5])
            def _():
                second_copy(x, me, source).wait_recv()

            return carry

        lax.fori_loop(1, n, second_wait, 0)

    xn_lo = lo + 1 - 2 * lax.rem(lo, 2)
    yn_lo = lax.rem(lo + 2, PLANE)
    dn_lo = PLANE - 1 - lo
    held = ((kb0, kb1), (vb0, vb1))

    def need(s, source, dest):
        if s == 0:
            return source < dest
        if s == back:
            return source > dest
        return source >= 0

    def z_copy(t, part, s):
        ref = held[t][part]
        return pltpu.make_async_remote_copy(
            src_ref=ref.at[s, lo],
            dst_ref=ref.at[s + 1, lo],
            send_sem=zs_sem.at[t, part, s],
            recv_sem=zr_sem.at[t, part, s + 1],
            device_id=(lax.rem(me + PLANE, n), tp),
            device_id_type=MESH,
        )

    def p_copy(t, kind, s, block, part, dest):
        ref = held[t][part]
        return pltpu.make_async_remote_copy(
            src_ref=ref.at[s, block],
            dst_ref=ref.at[s, block],
            send_sem=ps_sem.at[t, kind, s],
            recv_sem=pr_sem.at[t, kind, s],
            device_id=(hi * PLANE + dest, tp),
            device_id_type=MESH,
        )

    def plan(s, sender, x_of, y_of, d_of):
        return (
            (0, sender, 0, x_of, need(s, sender, x_of)),
            (1, sender, 1, x_of, need(s, sender, x_of) | need(s, sender, d_of)),
            (2, sender, 0, y_of, need(s, sender, y_of) | need(s, sender, d_of)),
            (3, sender, 1, y_of, need(s, sender, y_of)),
        )

    def relays(s):
        return (
            (4, yn_lo, 0, xn_lo, need(s, yn_lo, xn_lo)),
            (5, xn_lo, 1, yn_lo, need(s, xn_lo, yn_lo)),
        )

    def launch(t, s):
        if s < back:

            @pl.when((hi >= s) & (hi + 1 < planes))
            def _():
                z_copy(t, 0, s).start()
                z_copy(t, 1, s).start()

        first, second, third, fourth = plan(s, lo, xn_lo, yn_lo, dn_lo)
        for kind, block, part, dest, wanted in (second, third, first, fourth):

            @pl.when((hi >= s) & wanted)
            def _():
                p_copy(t, kind, s, block, part, dest).start()

    def arrive(t, s):
        from_x = plan(s, xn_lo, lo, dn_lo, yn_lo)[:2]
        from_y = plan(s, yn_lo, dn_lo, lo, xn_lo)[2:]
        for (kind, block, part, dest, wanted), relay in zip(
            (from_y[0], from_x[1], from_x[0], from_y[1]), relays(s) + (None, None)
        ):

            @pl.when((hi >= s) & wanted)
            def _():
                p_copy(t, kind, s, block, part, dest).wait_recv()

            if relay is not None:
                r_kind, r_block, r_part, r_dest, r_wanted = relay

                @pl.when((hi >= s) & r_wanted)
                def _():
                    p_copy(t, r_kind, s, r_block, r_part, r_dest).start()

    def diagonal(t, s):
        @pl.when((hi >= s) & need(s, dn_lo, lo))
        def _():
            p_copy(t, 4, s, dn_lo, 0, lo).wait_recv()
            p_copy(t, 5, s, dn_lo, 1, lo).wait_recv()

    def step(t, s):
        @pl.when(hi >= s)
        def _():
            z_copy(t, 0, s - 1).wait_recv()
            z_copy(t, 1, s - 1).wait_recv()

        launch(t, s)

    second_phase(0)
    launch(1, 0)

    if dseg > lw:
        xown[...] = jnp.zeros_like(xown)
    for k in range(tpn):

        @pl.when(tp == k)
        def _():
            xown[:, :lw] = xn[:, k * lw : (k + 1) * lw]

    dmaps[...] = jnp.zeros_like(dmaps)
    kv_copy(0).wait()
    plain_k[...] = jnp.dot(xn[...], wkv[0], preferred_element_type=jnp.float32)
    second_phase(1)

    row_pos = me * rows + lax.broadcasted_iota(jnp.int32, (rows, hw), 0)
    row_start = jnp.zeros((rows, hw), jnp.int32)
    for j in range(count):
        row_start = row_start + jnp.where(ends[j] <= row_pos, lengths[j], 0)
    angles = (row_pos - row_start).astype(jnp.float32) * freq_ref[...]
    sine = jnp.sin(angles)
    cos_t[...] = jnp.cos(angles)
    lane = lax.broadcasted_iota(jnp.int32, (rows, hw), 1)
    sin_t[...] = jnp.where(lane < hw // 2, -sine, sine)
    acc[...] = jnp.zeros_like(acc)
    accl[...] = jnp.zeros_like(accl)
    accd[...] = jnp.zeros_like(accd)

    def low_copy(x, k, source):
        return pltpu.make_async_remote_copy(
            src_ref=lowp.at[x],
            dst_ref=lowr.at[x, source],
            send_sem=sl_sem.at[x, k],
            recv_sem=rl_sem.at[x, source],
            device_id=(me, lax.rem(tp + k, tpn)),
            device_id_type=MESH,
        )

    def low_send(x, maps, parts):
        for u in range(units):
            for r in range(parts):
                dmaps[x, u, r * rank : (r + 1) * rank, :] = maps[u, :, r * dseg : (r + 1) * dseg]
            rows_u = slice(u * SHORT_LEN, (u + 1) * SHORT_LEN)
            lowp[x, rows_u, :] = nt_dot(xown[rows_u, :], dmaps[x, u])
        for k in range(1, tpn):
            low_copy(x, k, tp).start()

    def low_sum(x):
        low = lowp[x]
        for k in range(1, tpn):
            source = lax.rem(tp + k, tpn)
            low_copy(x, tpn - k, source).wait_recv()
            low = low + lowr[x, source]
        return low

    def increment(low, maps, start, width):
        return jnp.concatenate(
            [
                jnp.dot(
                    low[u * SHORT_LEN : (u + 1) * SHORT_LEN, :rank],
                    maps[u, :, pl.ds(start, width)],
                    preferred_element_type=jnp.float32,
                )
                for u in range(units)
            ],
            0,
        )

    def head(values, gain):
        inverse = lax.rsqrt(jnp.mean(values * values, axis=-1, keepdims=True) + EPSILON)
        values = values * inverse * gain
        return (values * cos_t[...] + pltpu.roll(values, hw // 2, 1) * sin_t[...]).astype(
            jnp.bfloat16
        )

    step(1, 1)
    arrive(1, 0)

    def q_product(c, carry):
        q_copy(c).wait()
        plain_q[c] = jnp.dot(xn[...], wq[c], preferred_element_type=jnp.float32)
        return carry

    lax.fori_loop(0, nkv, q_product, 0)

    second_arrival(0)
    low_send(0, maps_a, 2)
    low_kv = low_sum(0)
    kb0[0, lo, half_rows:, :rows] = low_kv.T[rank : 2 * rank, :].astype(jnp.bfloat16)
    kgain = kgain_ref[...].astype(jnp.float32)
    qgain = qgain_ref[...].astype(jnp.float32)
    k_raw = plain_k[...] + ADAPTER_SCALE * increment(
        low_kv.astype(jnp.bfloat16), maps_a, k_at, kvw
    )
    for k in range(nkv):
        cols = slice(k * hw, (k + 1) * hw)
        key = head(k_raw[:, cols], kgain)
        kb0[0, lo, :half_rows, cols] = key[:half_rows]
        kb1[0, lo, :, cols] = key[half_rows:]
    launch(0, 0)
    for s in range(2, back + 1):
        step(1, s)
        arrive(1, s - 1)

    second_arrival(1)
    low_send(1, maps_b, 1)
    low_q = low_sum(1).astype(jnp.bfloat16)

    def q_final(c, carry):
        start = pl.multiple_of(q_at + c * gw, 128)
        raw = plain_q[c] + ADAPTER_SCALE * increment(low_q, maps_b, start, gw)
        for g in range(group):
            qbuf[c, g * rows : (g + 1) * rows, :] = head(raw[:, g * hw : (g + 1) * hw], qgain)
        return carry

    lax.fori_loop(0, nkv, q_final, 0)

    factor = math.log2(math.e) / math.sqrt(hw)

    def attend(s, block, wanted):
        @pl.when((hi >= s) & wanted)
        def _():
            key_pos = ((hi - s) * PLANE + block) * rows + lax.broadcasted_iota(
                jnp.int32, (rows, rows), 1
            )
            query_pos = me * rows + lax.broadcasted_iota(jnp.int32, (rows, rows), 0)
            first = jnp.zeros((rows, rows), jnp.int32)
            for j in range(count):
                first = first + jnp.where(ends[j] <= query_pos, lengths[j], 0)
            bias = jnp.where((key_pos >= first) & (key_pos <= query_pos), 0.0, MASKED)
            bias = jnp.concatenate([bias] * group, 0)
            low_v = kb0[s, block, half_rows:, :rows]
            for k in range(nkv):
                cols = slice(k * hw, (k + 1) * hw)
                key = jnp.concatenate([kb0[s, block, :half_rows, cols], kb1[s, block, :, cols]], 0)
                value = jnp.concatenate([vb0[s, block, :, cols], vb1[s, block, :, cols]], 0)
                weights = jnp.exp2(nt_dot(qbuf[k], key) * factor + bias)
                accl[k] += weights
                weights = weights.astype(jnp.bfloat16)
                acc[k] += jnp.dot(weights, value, preferred_element_type=jnp.float32)
                accd[k] += nt_dot(weights, low_v)

    for s in range(back + 1):
        if s < back:
            step(0, s + 1)
        arrive(0, s)
        if s == back:
            arrive(1, s)
        if s == 0:
            attend(0, lo, lo >= 0)
        else:
            attend(s, lo, lo >= 0)
        attend(s, xn_lo, need(s, xn_lo, lo))
        attend(s, yn_lo, need(s, yn_lo, lo))
        if s >= 1:
            diagonal(1, s - 1)
            diagonal(0, s - 1)
            attend(s - 1, dn_lo, need(s - 1, dn_lo, lo))
    diagonal(1, back)
    diagonal(0, back)
    attend(back, dn_lo, need(back, dn_lo, lo))

    unit_of = lax.div(
        lax.rem(lax.broadcasted_iota(jnp.int32, (group * rows, hw), 0), rows), SHORT_LEN
    )
    for k in range(nkv):
        total = jnp.sum(accl[k], axis=-1, keepdims=True)
        low_mean = (accd[k] / total).astype(jnp.bfloat16)
        extra = jnp.zeros((group * rows, hw), jnp.float32)
        for u in range(units):
            up = maps_b[u, :, v_at + k * hw : v_at + (k + 1) * hw]
            extra = jnp.where(
                unit_of == u, jnp.dot(low_mean, up, preferred_element_type=jnp.float32), extra
            )
        result = (acc[k] / total + ADAPTER_SCALE * extra).astype(out_ref.dtype)
        for g in range(group):
            at = (k * group + g) * hw
            out_ref[:, at : at + hw] = result[g * rows : (g + 1) * rows, :]

    def drain(k, carry):
        dest = lax.rem(me + k, n)
        for x in range(2):

            @pl.when(dest < groups[x][5])
            def _():
                first_copy(x, dest, me).wait_send()

            @pl.when(me < groups[x][5])
            def _():
                second_copy(x, dest, me).wait_send()

        return carry

    lax.fori_loop(1, n, drain, 0)
    for x in range(2):
        for k in range(1, tpn):
            low_copy(x, k, tp).wait_send()
    for t in range(2):
        for s in range(back + 1):
            if s < back:

                @pl.when((hi >= s) & (hi + 1 < planes))
                def _():
                    z_copy(t, 0, s).wait_send()
                    z_copy(t, 1, s).wait_send()

            for kind, block, part, dest, wanted in (
                plan(s, lo, xn_lo, yn_lo, dn_lo) + relays(s)
            ):

                @pl.when((hi >= s) & wanted)
                def _():
                    p_copy(t, kind, s, block, part, dest).wait_send()


def on_device(
    n,
    tpn,
    tokens,
    input_norm_gain,
    query_weight,
    key_value_weight,
    query_head_gain,
    key_head_gain,
    adapter_down_maps,
    query_up_maps,
    key_value_up_maps,
    packed_lengths,
    adapter_per_prompt,
    adapter_place,
):
    rows, width = tokens.shape
    hw = query_head_gain.shape[0]
    nkv = key_value_weight.shape[2] // hw
    group = query_weight.shape[1] // hw // nkv
    rank, lw = query_up_maps.shape[1], adapter_down_maps.shape[2]
    units = rows // SHORT_LEN
    dseg = -(-lw // 128) * 128
    kvw, gw = nkv * hw, group * hw

    def pieces_of(used):
        piece = -(-(used // 128) // n) * 128
        return piece, -(-used // piece)

    piece_a, pieces_a = pieces_of(2 * dseg + kvw)
    piece_b, pieces_b = pieces_of(dseg + nkv * gw + kvw)
    back = n // 2 // PLANE
    cfg = dict(
        n=n,
        tpn=tpn,
        rows=rows,
        units=units,
        rank=rank,
        lw=lw,
        dseg=dseg,
        piece_a=piece_a,
        pieces_a=pieces_a,
        piece_b=piece_b,
        pieces_b=pieces_b,
        count=packed_lengths.shape[0],
        nkv=nkv,
        group=group,
        hw=hw,
    )
    powers = np.arange(hw // 2, dtype=np.float64) * (2.0 / hw)
    frequency = (THETA ** (-powers)).astype(np.float32)
    frequency = jnp.asarray(np.concatenate([frequency, frequency])[None, :])
    vmem = pl.BlockSpec(memory_space=pltpu.VMEM)
    hbm = pl.BlockSpec(memory_space=pltpu.HBM)
    bf, f32 = jnp.bfloat16, jnp.float32
    dma = pltpu.SemaphoreType.DMA
    call = pl.pallas_call(
        functools.partial(fused_kernel, cfg),
        out_shape=jax.ShapeDtypeStruct((rows, nkv * gw), bf),
        in_specs=[hbm] * 13,
        out_specs=vmem,
        scratch_shapes=[
            pltpu.SMEM(packed_lengths.shape, jnp.int32),
            pltpu.SMEM(adapter_per_prompt.shape, jnp.int32),
            pltpu.SMEM(adapter_place.shape, jnp.int32),
            pltpu.VMEM((rows, width), bf),
            pltpu.VMEM((1, width), bf),
            pltpu.VMEM((1, hw), bf),
            pltpu.VMEM((1, hw), bf),
            pltpu.VMEM((1, hw), f32),
            pltpu.VMEM(adapter_down_maps.shape, bf),
            pltpu.VMEM(query_up_maps.shape, bf),
            pltpu.VMEM(key_value_up_maps.shape, bf),
            pltpu.VMEM((nkv, width, gw), bf),
            pltpu.VMEM((2, width, kvw), bf),
            pltpu.VMEM((rows, width), bf),
            pltpu.VMEM((rows, dseg), bf),
            pltpu.VMEM((rank, pieces_a * piece_a), bf),
            pltpu.VMEM((rank, pieces_b * piece_b), bf),
            pltpu.VMEM((n, rank, piece_a), bf),
            pltpu.VMEM((n, rank, piece_b), bf),
            pltpu.VMEM((n, units, rank, piece_a), bf),
            pltpu.VMEM((n, units, rank, piece_b), bf),
            pltpu.VMEM((units, rank, pieces_a * piece_a), bf),
            pltpu.VMEM((units, rank, pieces_b * piece_b), bf),
            pltpu.VMEM((2, units, 128, dseg), bf),
            pltpu.VMEM((2, rows, 128), f32),
            pltpu.VMEM((2, tpn, rows, 128), f32),
            pltpu.VMEM((nkv, rows, gw), f32),
            pltpu.VMEM((rows, kvw), f32),
            pltpu.VMEM((nkv, group * rows, hw), bf),
            pltpu.VMEM((back + 1, PLANE, rows // 2 + rank, kvw), bf),
            pltpu.VMEM((back + 1, PLANE, rows // 2, kvw), bf),
            pltpu.VMEM((back + 1, PLANE, rows // 2, kvw), bf),
            pltpu.VMEM((back + 1, PLANE, rows // 2, kvw), bf),
            pltpu.VMEM((nkv, group * rows, hw), f32),
            pltpu.VMEM((nkv, group * rows, rows), f32),
            pltpu.VMEM((nkv, group * rows, rank), f32),
            pltpu.VMEM((rows, hw), f32),
            pltpu.VMEM((rows, hw), f32),
            dma((11,)),
            dma((nkv,)),
            dma((2,)),
            dma((2, n)),
            dma((2, n)),
            dma((2, n)),
            dma((2, n)),
            dma((2, tpn)),
            dma((2, tpn)),
            dma((2, 2, back + 1)),
            dma((2, 2, back + 1)),
            dma((2, 6, back + 1)),
            dma((2, 6, back + 1)),
        ],
        compiler_params=pltpu.CompilerParams(
            collective_id=0, has_side_effects=True, vmem_limit_bytes=56 << 20
        ),
    )
    return call(
        packed_lengths,
        adapter_per_prompt,
        adapter_place,
        tokens,
        input_norm_gain.reshape(1, -1),
        query_head_gain.reshape(1, -1),
        key_head_gain.reshape(1, -1),
        frequency,
        adapter_down_maps,
        query_up_maps,
        key_value_up_maps,
        query_weight,
        key_value_weight,
    )


def solution(mesh):
    in_specs = (
        P("req", None),
        P(),
        P(None, "tp"),
        P(None, None, "tp"),
        P(),
        P(),
        P("req", None, "tp"),
        P("req", None, "tp"),
        P("req", None, None, "tp"),
        P(),
        P(),
        P(),
    )
    body = functools.partial(on_device, mesh.shape["req"], mesh.shape["tp"])
    return jax.shard_map(
        body, mesh=mesh, in_specs=in_specs, out_specs=P("req", "tp"), check_vma=False
    )
```

```python
import functools
import math

import jax
import jax.numpy as jnp
import numpy as np
from jax import lax
from jax.experimental import pallas as pl
from jax.experimental.pallas import tpu as pltpu
from jax.sharding import PartitionSpec as P

SHORT_LEN = 64
PLANE = 4
EPSILON = 1e-06
THETA = 1000000.0
ADAPTER_SCALE = 2.0
MASKED = -1e30
MESH = pl.DeviceIdType.MESH


def nt_dot(left, right):
    return lax.dot_general(
        left, right, (((1,), (1,)), ((), ())), preferred_element_type=jnp.float32
    )


def fused_kernel(
    cfg,
    lengths_hbm,
    prompt_adapter_hbm,
    place_hbm,
    tokens_hbm,
    gain_hbm,
    qgain_hbm,
    kgain_hbm,
    freq_hbm,
    down_hbm,
    upq_hbm,
    upkv_hbm,
    wq_hbm,
    wkv_hbm,
    out_ref,
    lengths_ref,
    prompt_adapter_ref,
    place_ref,
    tokens_ref,
    gain_ref,
    qgain_ref,
    kgain_ref,
    freq_ref,
    down_ref,
    upq_ref,
    upkv_ref,
    wq,
    wkv,
    xn,
    xown,
    slab_a,
    slab_b,
    part_a,
    part_b,
    stage_a,
    stage_b,
    maps_a,
    maps_b,
    dmaps,
    lowp,
    lowr,
    plain_q,
    plain_k,
    qbuf,
    kb0,
    kb1,
    vb0,
    vb1,
    acc,
    accl,
    accd,
    cos_t,
    sin_t,
    in_sem,
    wq_sem,
    wkv_sem,
    s1_sem,
    r1_sem,
    s2_sem,
    r2_sem,
    sl_sem,
    rl_sem,
    zs_sem,
    zr_sem,
    ps_sem,
    pr_sem,
):
    n, tpn, rows, units = cfg["n"], cfg["tpn"], cfg["rows"], cfg["units"]
    rank, lw, dseg = cfg["rank"], cfg["lw"], cfg["dseg"]
    nkv, group, hw = cfg["nkv"], cfg["group"], cfg["hw"]
    kvw, gw, half_rows = nkv * hw, group * hw, rows // 2
    planes, back = n // PLANE, n // 2 // PLANE
    me = lax.axis_index("req")
    tp = lax.axis_index("tp")
    hi = lax.div(me, PLANE)
    lo = lax.rem(me, PLANE)

    def q_copy(c):
        return pltpu.make_async_copy(
            wq_hbm.at[:, pl.ds(pl.multiple_of(c * gw, 128), gw)], wq.at[c], wq_sem.at[c]
        )

    def kv_copy(c):
        return pltpu.make_async_copy(wkv_hbm.at[c], wkv.at[c], wkv_sem.at[c])

    loads = [
        pltpu.make_async_copy(source, dest, in_sem.at[i])
        for i, (source, dest) in enumerate(
            (
                (down_hbm, down_ref),
                (upkv_hbm, upkv_ref),
                (upq_hbm, upq_ref),
                (tokens_hbm, tokens_ref),
                (gain_hbm, gain_ref),
                (lengths_hbm, lengths_ref),
                (prompt_adapter_hbm, prompt_adapter_ref),
                (place_hbm, place_ref),
                (freq_hbm, freq_ref),
                (qgain_hbm, qgain_ref),
                (kgain_hbm, kgain_ref),
            )
        )
    ]
    for load in loads:
        load.start()
    kv_copy(1).start()
    kv_copy(0).start()
    for c in range(nkv):
        q_copy(c).start()

    barrier = pltpu.get_barrier_semaphore()

    def greet(k, carry):
        pl.semaphore_signal(
            barrier, inc=1, device_id=(lax.rem(me + k, n), tp), device_id_type=MESH
        )
        return carry

    lax.fori_loop(1, n, greet, 0)
    for k in range(1, tpn):
        pl.semaphore_signal(
            barrier, inc=1, device_id=(me, lax.rem(tp + k, tpn)), device_id_type=MESH
        )
    for load in loads[:3]:
        load.wait()

    slab_a[...] = jnp.zeros_like(slab_a)
    slab_b[...] = jnp.zeros_like(slab_b)
    slab_b[:, :lw] = down_ref[0, :rank, :]
    slab_a[:, :lw] = down_ref[0, rank : 2 * rank, :]
    slab_a[:, dseg : dseg + lw] = down_ref[0, 2 * rank : 3 * rank, :]
    k_at, q_at = 2 * dseg, dseg
    v_at = q_at + nkv * gw
    slab_a[:, k_at : k_at + kvw] = upkv_ref[0, 0]
    slab_b[:, q_at : q_at + nkv * gw] = upq_ref[0]
    slab_b[:, v_at : v_at + kvw] = upkv_ref[0, 1]

    pl.semaphore_wait(barrier, n - 1 + tpn - 1)

    groups = (
        (slab_a, part_a, stage_a, maps_a, cfg["piece_a"], cfg["pieces_a"]),
        (slab_b, part_b, stage_b, maps_b, cfg["piece_b"], cfg["pieces_b"]),
    )

    def lanes(index, piece):
        return pl.ds(pl.multiple_of(index * piece, 128), piece)

    def first_copy(x, dest, source):
        slab, part, _, _, piece, _ = groups[x]
        return pltpu.make_async_remote_copy(
            src_ref=slab.at[:, lanes(dest, piece)],
            dst_ref=part.at[source],
            send_sem=s1_sem.at[x, dest],
            recv_sem=r1_sem.at[x, source],
            device_id=(dest, tp),
            device_id_type=MESH,
        )

    def first_phase(x):
        def first_send(k, carry):
            dest = lax.rem(me + k, n)

            @pl.when(dest < groups[x][5])
            def _():
                first_copy(x, dest, me).start()

            return carry

        lax.fori_loop(1, n, first_send, 0)

    first_phase(0)
    first_phase(1)

    for load in loads[3:]:
        load.wait()
    count = cfg["count"]
    lengths = [lengths_ref[j] for j in range(count)]
    ends = []
    running = jnp.int32(0)
    for j in range(count):
        running = running + lengths[j]
        ends.append(running)

    values = tokens_ref[...].astype(jnp.float32)
    inverse = lax.rsqrt(jnp.mean(values * values, axis=-1, keepdims=True) + EPSILON)
    xn[...] = (values * inverse * gain_ref[...].astype(jnp.float32).reshape(1, -1)).astype(jnp.bfloat16)
    kv_copy(1).wait()
    plain_v = jnp.dot(xn[...], wkv[1], preferred_element_type=jnp.float32).astype(jnp.bfloat16)
    vb0[0, lo] = plain_v[:half_rows]
    vb1[0, lo] = plain_v[half_rows:]

    def slot_of(position):
        prompt = jnp.int32(0)
        for j in range(count - 1):
            prompt = prompt + (ends[j] <= position).astype(jnp.int32)
        return place_ref[prompt_adapter_ref[prompt]]

    def second_copy(x, dest, source):
        _, _, stage, maps, piece, _ = groups[x]
        return pltpu.make_async_remote_copy(
            src_ref=stage.at[dest],
            dst_ref=maps.at[:, :, lanes(source, piece)],
            send_sem=s2_sem.at[x, dest],
            recv_sem=r2_sem.at[x, source],
            device_id=(dest, tp),
            device_id_type=MESH,
        )

    def second_phase(x):
        slab, part, stage, maps, piece, pieces = groups[x]

        @pl.when(me < pieces)
        def _():
            part[me] = slab[:, lanes(me, piece)]

            def first_wait(k, carry):
                first_copy(x, me, lax.rem(me + k, n)).wait_recv()
                return carry

            lax.fori_loop(1, n, first_wait, 0)

            def second_send(k, carry):
                dest = lax.rem(me + k, n)
                for u in range(units):
                    stage[dest, u] = part[slot_of((dest * units + u) * SHORT_LEN)]
                second_copy(x, dest, me).start()
                return carry

            lax.fori_loop(1, n, second_send, 0)
            for u in range(units):
                maps[u, :, lanes(me, piece)] = part[slot_of((me * units + u) * SHORT_LEN)]

    def second_arrival(x):
        def second_wait(k, carry):
            source = lax.rem(me + k, n)

            @pl.when(source < groups[x][5])
            def _():
                second_copy(x, me, source).wait_recv()

            return carry

        lax.fori_loop(1, n, second_wait, 0)

    xn_lo = lo + 1 - 2 * lax.rem(lo, 2)
    yn_lo = lax.rem(lo + 2, PLANE)
    dn_lo = PLANE - 1 - lo
    held = ((kb0, kb1), (vb0, vb1))

    def need(s, source, dest):
        if s == 0:
            return source < dest
        if s == back:
            return source > dest
        return source >= 0

    def z_copy(t, part, s):
        ref = held[t][part]
        return pltpu.make_async_remote_copy(
            src_ref=ref.at[s, lo],
            dst_ref=ref.at[s + 1, lo],
            send_sem=zs_sem.at[t, part, s],
            recv_sem=zr_sem.at[t, part, s + 1],
            device_id=(lax.rem(me + PLANE, n), tp),
            device_id_type=MESH,
        )

    def p_copy(t, kind, s, block, part, dest):
        ref = held[t][part]
        return pltpu.make_async_remote_copy(
            src_ref=ref.at[s, block],
            dst_ref=ref.at[s, block],
            send_sem=ps_sem.at[t, kind, s],
            recv_sem=pr_sem.at[t, kind, s],
            device_id=(hi * PLANE + dest, tp),
            device_id_type=MESH,
        )

    def plan(s, sender, x_of, y_of, d_of):
        return (
            (0, sender, 0, x_of, need(s, sender, x_of)),
            (1, sender, 1, x_of, need(s, sender, x_of) | need(s, sender, d_of)),
            (2, sender, 0, y_of, need(s, sender, y_of) | need(s, sender, d_of)),
            (3, sender, 1, y_of, need(s, sender, y_of)),
        )

    def relays(s):
        return (
            (4, yn_lo, 0, xn_lo, need(s, yn_lo, xn_lo)),
            (5, xn_lo, 1, yn_lo, need(s, xn_lo, yn_lo)),
        )

    def launch(t, s):
        if s < back:

            @pl.when((hi >= s) & (hi + 1 < planes))
            def _():
                z_copy(t, 0, s).start()
                z_copy(t, 1, s).start()

        first, second, third, fourth = plan(s, lo, xn_lo, yn_lo, dn_lo)
        for kind, block, part, dest, wanted in (second, third, first, fourth):

            @pl.when((hi >= s) & wanted)
            def _():
                p_copy(t, kind, s, block, part, dest).start()

    def arrive(t, s):
        from_x = plan(s, xn_lo, lo, dn_lo, yn_lo)[:2]
        from_y = plan(s, yn_lo, dn_lo, lo, xn_lo)[2:]
        for (kind, block, part, dest, wanted), relay in zip(
            (from_y[0], from_x[1], from_x[0], from_y[1]), relays(s) + (None, None)
        ):

            @pl.when((hi >= s) & wanted)
            def _():
                p_copy(t, kind, s, block, part, dest).wait_recv()

            if relay is not None:
                r_kind, r_block, r_part, r_dest, r_wanted = relay

                @pl.when((hi >= s) & r_wanted)
                def _():
                    p_copy(t, r_kind, s, r_block, r_part, r_dest).start()

    def diagonal(t, s):
        @pl.when((hi >= s) & need(s, dn_lo, lo))
        def _():
            p_copy(t, 4, s, dn_lo, 0, lo).wait_recv()
            p_copy(t, 5, s, dn_lo, 1, lo).wait_recv()

    def step(t, s):
        @pl.when(hi >= s)
        def _():
            z_copy(t, 0, s - 1).wait_recv()
            z_copy(t, 1, s - 1).wait_recv()

        launch(t, s)

    second_phase(0)
    launch(1, 0)

    if dseg > lw:
        xown[...] = jnp.zeros_like(xown)
    for k in range(tpn):

        @pl.when(tp == k)
        def _():
            xown[:, :lw] = xn[:, k * lw : (k + 1) * lw]

    dmaps[...] = jnp.zeros_like(dmaps)
    kv_copy(0).wait()
    plain_k[...] = jnp.dot(xn[...], wkv[0], preferred_element_type=jnp.float32)
    second_phase(1)

    row_pos = me * rows + lax.broadcasted_iota(jnp.int32, (rows, hw), 0)
    row_start = jnp.zeros((rows, hw), jnp.int32)
    for j in range(count):
        row_start = row_start + jnp.where(ends[j] <= row_pos, lengths[j], 0)
    angles = (row_pos - row_start).astype(jnp.float32) * freq_ref[...]
    sine = jnp.sin(angles)
    cos_t[...] = jnp.cos(angles)
    lane = lax.broadcasted_iota(jnp.int32, (rows, hw), 1)
    sin_t[...] = jnp.where(lane < hw // 2, -sine, sine)
    acc[...] = jnp.zeros_like(acc)
    accl[...] = jnp.zeros_like(accl)
    accd[...] = jnp.zeros_like(accd)

    def low_copy(x, k, source):
        return pltpu.make_async_remote_copy(
            src_ref=lowp.at[x],
            dst_ref=lowr.at[x, source],
            send_sem=sl_sem.at[x, k],
            recv_sem=rl_sem.at[x, source],
            device_id=(me, lax.rem(tp + k, tpn)),
            device_id_type=MESH,
        )

    def low_send(x, maps, parts):
        for u in range(units):
            for r in range(parts):
                dmaps[x, u, r * rank : (r + 1) * rank, :] = maps[u, :, r * dseg : (r + 1) * dseg]
            rows_u = slice(u * SHORT_LEN, (u + 1) * SHORT_LEN)
            lowp[x, rows_u, :] = nt_dot(xown[rows_u, :], dmaps[x, u])
        for k in range(1, tpn):
            low_copy(x, k, tp).start()

    def low_sum(x):
        low = lowp[x]
        for k in range(1, tpn):
            source = lax.rem(tp + k, tpn)
            low_copy(x, tpn - k, source).wait_recv()
            low = low + lowr[x, source]
        return low

    def increment(low, maps, start, width):
        return jnp.concatenate(
            [
                jnp.dot(
                    low[u * SHORT_LEN : (u + 1) * SHORT_LEN, :rank],
                    maps[u, :, pl.ds(start, width)],
                    preferred_element_type=jnp.float32,
                )
                for u in range(units)
            ],
            0,
        )

    def head(values, gain):
        inverse = lax.rsqrt(jnp.mean(values * values, axis=-1, keepdims=True) + EPSILON)
        values = values * inverse * gain
        return (values * cos_t[...] + pltpu.roll(values, hw // 2, 1) * sin_t[...]).astype(
            jnp.bfloat16
        )

    step(1, 1)
    arrive(1, 0)

    def q_product(c, carry):
        q_copy(c).wait()
        plain_q[c] = jnp.dot(xn[...], wq[c], preferred_element_type=jnp.float32)
        return carry

    lax.fori_loop(0, nkv, q_product, 0)

    second_arrival(0)
    low_send(0, maps_a, 2)
    low_kv = low_sum(0)
    kb0[0, lo, half_rows:, :rows] = low_kv.T[rank : 2 * rank, :].astype(jnp.bfloat16)
    kgain = kgain_ref[...].astype(jnp.float32)
    qgain = qgain_ref[...].astype(jnp.float32)
    k_raw = plain_k[...] + ADAPTER_SCALE * increment(
        low_kv.astype(jnp.bfloat16), maps_a, k_at, kvw
    )
    for k in range(nkv):
        cols = slice(k * hw, (k + 1) * hw)
        key = head(k_raw[:, cols], kgain)
        kb0[0, lo, :half_rows, cols] = key[:half_rows]
        kb1[0, lo, :, cols] = key[half_rows:]
    launch(0, 0)
    for s in range(2, back + 1):
        step(1, s)
        arrive(1, s - 1)

    second_arrival(1)
    low_send(1, maps_b, 1)
    low_q = low_sum(1).astype(jnp.bfloat16)

    def q_final(c, carry):
        start = pl.multiple_of(q_at + c * gw, 128)
        raw = plain_q[c] + ADAPTER_SCALE * increment(low_q, maps_b, start, gw)
        for g in range(group):
            qbuf[c, g * rows : (g + 1) * rows, :] = head(raw[:, g * hw : (g + 1) * hw], qgain)
        return carry

    lax.fori_loop(0, nkv, q_final, 0)

    factor = math.log2(math.e) / math.sqrt(hw)

    def attend(s, block, wanted):
        @pl.when((hi >= s) & wanted)
        def _():
            key_pos = ((hi - s) * PLANE + block) * rows + lax.broadcasted_iota(
                jnp.int32, (rows, rows), 1
            )
            query_pos = me * rows + lax.broadcasted_iota(jnp.int32, (rows, rows), 0)
            first = jnp.zeros((rows, rows), jnp.int32)
            for j in range(count):
                first = first + jnp.where(ends[j] <= query_pos, lengths[j], 0)
            bias = jnp.where((key_pos >= first) & (key_pos <= query_pos), 0.0, MASKED)
            bias = jnp.concatenate([bias] * group, 0)
            low_v = kb0[s, block, half_rows:, :rows]
            for k in range(nkv):
                cols = slice(k * hw, (k + 1) * hw)
                key = jnp.concatenate([kb0[s, block, :half_rows, cols], kb1[s, block, :, cols]], 0)
                value = jnp.concatenate([vb0[s, block, :, cols], vb1[s, block, :, cols]], 0)
                weights = jnp.exp2(nt_dot(qbuf[k], key) * factor + bias)
                accl[k] += weights
                weights = weights.astype(jnp.bfloat16)
                acc[k] += jnp.dot(weights, value, preferred_element_type=jnp.float32)
                accd[k] += nt_dot(weights, low_v)

    for s in range(back + 1):
        if s < back:
            step(0, s + 1)
        arrive(0, s)
        if s == back:
            arrive(1, s)
        if s == 0:
            attend(0, lo, lo >= 0)
        else:
            attend(s, lo, lo >= 0)
        attend(s, xn_lo, need(s, xn_lo, lo))
        attend(s, yn_lo, need(s, yn_lo, lo))
        if s >= 1:
            diagonal(1, s - 1)
            diagonal(0, s - 1)
            attend(s - 1, dn_lo, need(s - 1, dn_lo, lo))
    diagonal(1, back)
    diagonal(0, back)
    attend(back, dn_lo, need(back, dn_lo, lo))

    unit_of = lax.div(
        lax.rem(lax.broadcasted_iota(jnp.int32, (group * rows, hw), 0), rows), SHORT_LEN
    )
    for k in range(nkv):
        total = jnp.sum(accl[k], axis=-1, keepdims=True)
        low_mean = (accd[k] / total).astype(jnp.bfloat16)
        extra = jnp.zeros((group * rows, hw), jnp.float32)
        for u in range(units):
            up = maps_b[u, :, v_at + k * hw : v_at + (k + 1) * hw]
            extra = jnp.where(
                unit_of == u, jnp.dot(low_mean, up, preferred_element_type=jnp.float32), extra
            )
        result = (acc[k] / total + ADAPTER_SCALE * extra).astype(out_ref.dtype)
        for g in range(group):
            at = (k * group + g) * hw
            out_ref[:, at : at + hw] = result[g * rows : (g + 1) * rows, :]

    def drain(k, carry):
        dest = lax.rem(me + k, n)
        for x in range(2):

            @pl.when(dest < groups[x][5])
            def _():
                first_copy(x, dest, me).wait_send()

            @pl.when(me < groups[x][5])
            def _():
                second_copy(x, dest, me).wait_send()

        return carry

    lax.fori_loop(1, n, drain, 0)
    for x in range(2):
        for k in range(1, tpn):
            low_copy(x, k, tp).wait_send()
    for t in range(2):
        for s in range(back + 1):
            if s < back:

                @pl.when((hi >= s) & (hi + 1 < planes))
                def _():
                    z_copy(t, 0, s).wait_send()
                    z_copy(t, 1, s).wait_send()

            for kind, block, part, dest, wanted in (
                plan(s, lo, xn_lo, yn_lo, dn_lo) + relays(s)
            ):

                @pl.when((hi >= s) & wanted)
                def _():
                    p_copy(t, kind, s, block, part, dest).wait_send()


def on_device(
    n,
    tpn,
    tokens,
    input_norm_gain,
    query_weight,
    key_value_weight,
    query_head_gain,
    key_head_gain,
    adapter_down_maps,
    query_up_maps,
    key_value_up_maps,
    packed_lengths,
    adapter_per_prompt,
    adapter_place,
):
    rows, width = tokens.shape
    hw = query_head_gain.shape[0]
    nkv = key_value_weight.shape[2] // hw
    group = query_weight.shape[1] // hw // nkv
    rank, lw = query_up_maps.shape[1], adapter_down_maps.shape[2]
    units = rows // SHORT_LEN
    dseg = -(-lw // 128) * 128
    kvw, gw = nkv * hw, group * hw

    def pieces_of(used):
        piece = -(-(used // 128) // n) * 128
        return piece, -(-used // piece)

    piece_a, pieces_a = pieces_of(2 * dseg + kvw)
    piece_b, pieces_b = pieces_of(dseg + nkv * gw + kvw)
    back = n // 2 // PLANE
    cfg = dict(
        n=n,
        tpn=tpn,
        rows=rows,
        units=units,
        rank=rank,
        lw=lw,
        dseg=dseg,
        piece_a=piece_a,
        pieces_a=pieces_a,
        piece_b=piece_b,
        pieces_b=pieces_b,
        count=packed_lengths.shape[0],
        nkv=nkv,
        group=group,
        hw=hw,
    )
    powers = np.arange(hw // 2, dtype=np.float64) * (2.0 / hw)
    frequency = (THETA ** (-powers)).astype(np.float32)
    frequency = jnp.asarray(np.concatenate([frequency, frequency])[None, :])
    vmem = pl.BlockSpec(memory_space=pltpu.VMEM)
    hbm = pl.BlockSpec(memory_space=pltpu.HBM)
    bf, f32 = jnp.bfloat16, jnp.float32
    dma = pltpu.SemaphoreType.DMA
    call = pl.pallas_call(
        functools.partial(fused_kernel, cfg),
        out_shape=jax.ShapeDtypeStruct((rows, nkv * gw), bf),
        in_specs=[hbm] * 13,
        out_specs=vmem,
        scratch_shapes=[
            pltpu.SMEM(packed_lengths.shape, jnp.int32),
            pltpu.SMEM(adapter_per_prompt.shape, jnp.int32),
            pltpu.SMEM(adapter_place.shape, jnp.int32),
            pltpu.VMEM((rows, width), bf),
            pltpu.VMEM((width,), bf),
            pltpu.VMEM((1, hw), bf),
            pltpu.VMEM((1, hw), bf),
            pltpu.VMEM((1, hw), f32),
            pltpu.VMEM(adapter_down_maps.shape, bf),
            pltpu.VMEM(query_up_maps.shape, bf),
            pltpu.VMEM(key_value_up_maps.shape, bf),
            pltpu.VMEM((nkv, width, gw), bf),
            pltpu.VMEM((2, width, kvw), bf),
            pltpu.VMEM((rows, width), bf),
            pltpu.VMEM((rows, dseg), bf),
            pltpu.VMEM((rank, pieces_a * piece_a), bf),
            pltpu.VMEM((rank, pieces_b * piece_b), bf),
            pltpu.VMEM((n, rank, piece_a), bf),
            pltpu.VMEM((n, rank, piece_b), bf),
            pltpu.VMEM((n, units, rank, piece_a), bf),
            pltpu.VMEM((n, units, rank, piece_b), bf),
            pltpu.VMEM((units, rank, pieces_a * piece_a), bf),
            pltpu.VMEM((units, rank, pieces_b * piece_b), bf),
            pltpu.VMEM((2, units, 128, dseg), bf),
            pltpu.VMEM((2, rows, 128), f32),
            pltpu.VMEM((2, tpn, rows, 128), f32),
            pltpu.VMEM((nkv, rows, gw), f32),
            pltpu.VMEM((rows, kvw), f32),
            pltpu.VMEM((nkv, group * rows, hw), bf),
            pltpu.VMEM((back + 1, PLANE, rows // 2 + rank, kvw), bf),
            pltpu.VMEM((back + 1, PLANE, rows // 2, kvw), bf),
            pltpu.VMEM((back + 1, PLANE, rows // 2, kvw), bf),
            pltpu.VMEM((back + 1, PLANE, rows // 2, kvw), bf),
            pltpu.VMEM((nkv, group * rows, hw), f32),
            pltpu.VMEM((nkv, group * rows, rows), f32),
            pltpu.VMEM((nkv, group * rows, rank), f32),
            pltpu.VMEM((rows, hw), f32),
            pltpu.VMEM((rows, hw), f32),
            dma((11,)),
            dma((nkv,)),
            dma((2,)),
            dma((2, n)),
            dma((2, n)),
            dma((2, n)),
            dma((2, n)),
            dma((2, tpn)),
            dma((2, tpn)),
            dma((2, 2, back + 1)),
            dma((2, 2, back + 1)),
            dma((2, 6, back + 1)),
            dma((2, 6, back + 1)),
        ],
        compiler_params=pltpu.CompilerParams(
            collective_id=0, has_side_effects=True, vmem_limit_bytes=56 << 20
        ),
    )
    return call(
        packed_lengths,
        adapter_per_prompt,
        adapter_place,
        tokens,
        input_norm_gain,
        query_head_gain.reshape(1, -1),
        key_head_gain.reshape(1, -1),
        frequency,
        adapter_down_maps,
        query_up_maps,
        key_value_up_maps,
        query_weight,
        key_value_weight,
    )


def solution(mesh):
    in_specs = (
        P("req", None),
        P(),
        P(None, "tp"),
        P(None, None, "tp"),
        P(),
        P(),
        P("req", None, "tp"),
        P("req", None, "tp"),
        P("req", None, None, "tp"),
        P(),
        P(),
        P(),
    )
    body = functools.partial(on_device, mesh.shape["req"], mesh.shape["tp"])
    return jax.shard_map(
        body, mesh=mesh, in_specs=in_specs, out_specs=P("req", "tp"), check_vma=False
    )
```
